512 devices in a mesh: dfa: 32 (over y, x, z_hi), hid: 16 (over z_lo, core).
Axes of the slice: x: 4, y: 4, z: 16 (z_hi: 2, z_lo: 8; z = z_hi * 8 + z_lo), core: 2. Of those that a mesh axis runs over, the one named last changes fastest.
Arguments:
- beta_last: bfloat16 [256, 32, 16, 64], P('dfa', None, 'hid'), may hold values from -6 to 6
- transition: bfloat16 [32, 16, 64, 32768], P(None, 'hid', None, 'dfa'), may hold values from -0.03125 to 0.03125
- emission: bfloat16 [64, 16, 2048], P(None, 'hid'), may hold values from 0.049804688 to 0.59765625
- successor: int32 [256, 8], replicated, may hold values from 0 to 255
- token_set: int32 [256, 8], replicated, may hold values from 0 to 63
Outputs:
- table: bfloat16 [2, 256, 32, 16, 64], P(None, 'dfa', None, 'hid')
The draws below stay inside these ranges and needn't reach their ends.
All inputs are finite; a program needn't handle non-finite values.
Results may differ from the reference program's by a relative error of at most 0.0056.
Values may be sent and summed in bfloat16 or wider, within the bound.
No kernel may reach another device: no remote copies, remote signals or barrier semaphores. Data moves between devices by JAX's collectives and lax.ppermute only.
A program may use at most 128 MiB of HBM per device.

```python
import math
import jax
import jax.numpy as jnp

Q = 256
H = 32768
NSET = 64
DEG = 8
POS = 2
HC = 64
HW = 2048
N_DFA = 32
N_HID = 16


def touch_ends(values, key, smallest, high):
    index_at = [jax.random.randint(jax.random.fold_in(key, axis), (), 0, length) for axis, length in enumerate(values.shape)]
    longest = values.shape.index(max(values.shape))
    beside = index_at[:longest] + [(index_at[longest] + 1) % values.shape[longest]] + index_at[longest + 1:]
    return values.at[tuple(index_at)].set(smallest).at[tuple(beside)].set(high)


def block_scale(stream_key, extent, shards, least, largest):
    def one(axis_at, parts):
        heights = jax.random.uniform(jax.random.fold_in(jax.random.fold_in(stream_key, 6), axis_at), (parts,), jnp.float32, least / len(shards), largest / len(shards))
        return jnp.repeat(jnp.exp(heights), extent[axis_at] // parts).reshape((-1,) + (1,) * (len(extent) - axis_at - 1))

    factor_of = one(*shards[0])
    for cut in shards[1:]:
        factor_of = factor_of * one(*cut)
    return factor_of


def bell_draw(own_key, shape, spread, most, pieces=(), kind=jnp.bfloat16):
    result = spread * jax.random.normal(own_key, shape, jnp.float32)
    if pieces:
        result = result * block_scale(own_key, shape, pieces, -0.22, 0.18)
    return jnp.clip(result, -most, most).astype(kind)


def setup_inputs(seed: int = 0) -> dict:
    streams_of = jax.random.split(jax.random.key(seed), 6)
    beta_last = bell_draw(streams_of[0], (Q, N_DFA, N_HID, HC), 1.0, 6.0, ((0, 32), (2, 16)))
    transition = bell_draw(streams_of[1], (N_DFA, N_HID, HC, H), H ** -0.5, 0.03125, ((1, 16), (3, 32)))
    emission = jnp.clip(jnp.exp(math.log(0.59765625) - 2.4849066 * jax.random.uniform(streams_of[2], (NSET, N_HID, HW), jnp.float32) ** block_scale(streams_of[2], (NSET, N_HID, HW), ((1, 16),), -0.2, 0.2)), 0.049804688, 0.59765625).astype(jnp.bfloat16)
    successor = touch_ends(jax.random.randint(streams_of[3], (Q, DEG), 0, Q), jax.random.fold_in(streams_of[3], 1), 0, Q - 1).astype(jnp.int32)
    token_set = touch_ends(jax.random.randint(streams_of[4], (Q, DEG), 0, NSET), jax.random.fold_in(streams_of[4], 1), 0, NSET - 1).astype(jnp.int32)
    return dict(beta_last=beta_last, transition=transition, emission=emission, successor=successor, token_set=token_set)


def reference(beta_last, transition, emission, successor, token_set):
    beta_now = beta_last.reshape(Q, H)
    trans_full = transition.reshape(H, H)
    emission_rows = emission.reshape(NSET, N_HID, N_DFA, HC).transpose(0, 2, 1, 3).reshape(NSET, H)
    results = []
    for position in range(POS):
        total = jnp.zeros((Q, H), jnp.float32)
        for column in range(DEG):
            picked = beta_now[successor[:, column]].astype(jnp.float32)
            weights = emission_rows[token_set[:, column]].astype(jnp.float32)
            total = total + weights * picked
        mixed_rows = total.astype(jnp.bfloat16)
        summed = jnp.dot(mixed_rows, trans_full, preferred_element_type=jnp.float32)
        beta_now = summed.astype(jnp.bfloat16)
        results = [beta_now] + results
    return jnp.stack(results).reshape(POS, Q, N_DFA, N_HID, HC)
```

```python
import jax
import jax.numpy as jnp
from jax import lax
from jax.experimental import pallas as pl
from jax.experimental.pallas import tpu as pltpu
from jax.sharding import Mesh, PartitionSpec as P

BF, F32 = jnp.bfloat16, jnp.float32
DEG, NSET = 8, 64
PLANE = ("y", "x")
VMEM_LIMIT = 40 * 1024 * 1024


def dot(a, b):
    return jnp.dot(a, b, preferred_element_type=F32)


def one_hot_lanes(column, width):
    rows = column.shape[0]
    return (lax.broadcasted_iota(jnp.int32, (rows, width), 1) == column).astype(BF)


def one_hot_rows(row, height):
    cols = row.shape[1]
    return (lax.broadcasted_iota(jnp.int32, (height, cols), 0) == row).astype(BF)


def first_kernel(beta_ref, trans_ref, emis_ref, succ_ref, sets_ref, out_ref, pick, choose, total):
    step = pl.program_id(0)
    states = beta_ref.shape[0]

    @pl.when(step == 0)
    def _():
        total[...] = jnp.zeros_like(total)
        for j in range(DEG):
            pick[j] = one_hot_lanes(succ_ref[:, j : j + 1], states)
            choose[j] = one_hot_lanes(sets_ref[:, j : j + 1], NSET)

    mixed = jnp.zeros(beta_ref.shape, F32)
    for j in range(DEG):
        mixed = mixed + dot(choose[j], emis_ref[...]) * dot(pick[j], beta_ref[...])
    total[...] += dot(mixed.astype(BF), trans_ref[...])

    @pl.when(step == pl.num_programs(0) - 1)
    def _():
        half = out_ref.shape[0] // 2
        whole = total[...].T.reshape(-1, 2, 64, states)
        for c in range(2):
            out_ref[c * half : (c + 1) * half] = whole[:, c].reshape(half, states)


def mix_and_multiply(beta, trans, emis, succ, sets):
    states, width = beta.shape
    outs = trans.shape[1]
    blk = 256
    return pl.pallas_call(
        first_kernel,
        grid=(width // blk,),
        out_shape=jax.ShapeDtypeStruct((outs, states), F32),
        in_specs=[
            pl.BlockSpec((states, blk), lambda i: (0, i)),
            pl.BlockSpec((blk, outs), lambda i: (i, 0)),
            pl.BlockSpec((NSET, blk), lambda i: (0, i)),
            pl.BlockSpec((states, DEG), lambda i: (0, 0)),
            pl.BlockSpec((states, DEG), lambda i: (0, 0)),
        ],
        out_specs=pl.BlockSpec((outs, states), lambda i: (0, 0)),
        scratch_shapes=[
            pltpu.VMEM((DEG, states, states), BF),
            pltpu.VMEM((DEG, states, NSET), BF),
            pltpu.VMEM((states, outs), F32),
        ],
        compiler_params=pltpu.CompilerParams(vmem_limit_bytes=VMEM_LIMIT),
        name="mix_multiply",
    )(beta, trans, emis, succ, sets)


def middle_kernel(parts_ref, emis_ref, succ_ref, sets_ref, beta_ref, mixed_ref):
    total = parts_ref[0].astype(F32)
    for i in range(1, parts_ref.shape[0]):
        total = total + parts_ref[i].astype(F32)
    beta = total.astype(BF)
    beta_ref[...] = beta
    states = beta.shape[1]
    mixed = jnp.zeros(beta.shape, F32)
    for j in range(DEG):
        weights = dot(emis_ref[...], one_hot_rows(sets_ref[j : j + 1], NSET))
        mixed = mixed + weights * dot(beta, one_hot_rows(succ_ref[j : j + 1], states))
    mixed_ref[...] = mixed.astype(BF)


def sum_and_mix(parts, emis, succ, sets):
    shape = jax.ShapeDtypeStruct(parts.shape[1:], BF)
    return pl.pallas_call(
        middle_kernel,
        out_shape=(shape, shape),
        compiler_params=pltpu.CompilerParams(vmem_limit_bytes=VMEM_LIMIT),
        name="sum_mix",
    )(parts, emis, succ, sets)


def last_kernel(parts_ref, later_ref, out_ref):
    total = parts_ref[0].astype(F32)
    for i in range(1, parts_ref.shape[0]):
        total = total + parts_ref[i].astype(F32)
    beta = total.astype(BF).astype(F32)
    out_ref[...] = jnp.concatenate([beta, later_ref[...].astype(F32)], 0).T.astype(BF)


def sum_and_join(parts, later):
    _, width, states = parts.shape
    return pl.pallas_call(
        last_kernel,
        out_shape=jax.ShapeDtypeStruct((states, 2 * width), BF),
        compiler_params=pltpu.CompilerParams(vmem_limit_bytes=VMEM_LIMIT),
        name="sum_join",
    )(parts, later)


def spread(x, axes, count):
    return lax.all_to_all(jnp.broadcast_to(x[None], (count,) + x.shape), axes, 0, 0)


def gather_states(x):
    pair = spread(x, "zh", 2)
    return spread(pair, PLANE, 16).reshape((-1,) + x.shape[1:])


def reduce_hid(partial):
    pair = lax.all_to_all(partial.reshape(2, 8, 64, -1), "c", 0, 0)
    mine = (pair[0] + pair[1]).astype(BF)
    return lax.all_to_all(mine, "zl", 0, 0)


def local(beta_last, transition, emission, successor, token_set):
    states, blocks, _, cells = beta_last.shape
    width = blocks * cells
    trans = transition.reshape(width, transition.shape[3])
    emis = emission.reshape(NSET, width)
    own = lax.axis_index("y") * 8 + lax.axis_index("x") * 2 + lax.axis_index("zh")
    emis_own = lax.dynamic_slice_in_dim(emis, own * cells, cells, 1).T
    succ_t, sets_t = successor.T, token_set.T

    beta = gather_states(beta_last.reshape(states, width))
    partial = mix_and_multiply(beta, trans, emis, successor, token_set)
    later, mixed = sum_and_mix(reduce_hid(partial), emis_own, succ_t, sets_t)
    mixed = gather_states(mixed)
    partial = lax.dot_general(trans, mixed, (((0,), (0,)), ((), ())), preferred_element_type=F32)
    partial = partial.reshape(8, 2, 64, -1).swapaxes(0, 1)
    joined = sum_and_join(reduce_hid(partial), later)
    moved = lax.all_to_all(joined.reshape(32, states, 2, cells), PLANE + ("zh",), 0, 0)
    return moved.transpose(2, 1, 0, 3).reshape(2, states, blocks, 1, cells)


def solution(mesh):
    fine = Mesh(mesh.devices.reshape(4, 4, 2, 8, 2), ("y", "x", "zh", "zl", "c"))
    dfa, hid = ("y", "x", "zh"), ("zl", "c")
    return jax.shard_map(
        local,
        mesh=fine,
        in_specs=(
            P(dfa, None, hid, None),
            P(None, hid, None, dfa),
            P(None, hid, None),
            P(),
            P(),
        ),
        out_specs=P(None, dfa, None, hid, None),
        check_vma=False,
    )
```

```python
import jax
import jax.numpy as jnp
from jax import lax
from jax.experimental import pallas as pl
from jax.experimental.pallas import tpu as pltpu
from jax.sharding import Mesh, PartitionSpec as P

BF, F32 = jnp.bfloat16, jnp.float32
DEG, NSET = 8, 64
PLANE = ("y", "x")
MIB = 1024 * 1024
BLK = 256
BIG = 45
WHOLE = pl.BlockSpec(memory_space=pltpu.VMEM)
SCALAR = pl.BlockSpec(memory_space=pltpu.SMEM)


def shape(dims, dtype=BF):
    return jax.ShapeDtypeStruct(dims, dtype)


def params(mib):
    return pltpu.CompilerParams(vmem_limit_bytes=mib * MIB)


def dot(a, b, dims=((1,), (0,))):
    return lax.dot_general(a, b, (dims, ((), ())), preferred_element_type=F32)


ROWS = ((1,), (1,))


def iota(dims, axis):
    return lax.broadcasted_iota(jnp.int32, dims, axis)


def rows_kernel(beta_ref, out_ref):
    for i in range(0, beta_ref.shape[1], 2):
        out_ref[:, i * 64 : (i + 2) * 64] = jnp.concatenate([beta_ref[:, i], beta_ref[:, i + 1]], 1)


def as_rows(beta):
    states, blocks, cells = beta.shape
    return pl.pallas_call(
        rows_kernel, out_shape=shape((states, blocks * cells)), compiler_params=params(16), name="as_rows"
    )(beta)


def pair_kernel(zh_ref, mine_ref, theirs_ref, out_ref):
    mine, theirs = mine_ref[...].astype(F32), theirs_ref[...].astype(F32)
    first = zh_ref[0] == 0
    both = jnp.concatenate([jnp.where(first, mine, theirs), jnp.where(first, theirs, mine)], 0).astype(BF)
    for i in range(out_ref.shape[0]):
        out_ref[i] = both


def pair_copies(zh, mine, theirs):
    states, width = mine.shape
    return pl.pallas_call(
        pair_kernel,
        out_shape=shape((16, 2 * states, width)),
        in_specs=[SCALAR, WHOLE, WHOLE],
        compiler_params=params(16),
        name="pair_copies",
    )(zh, mine, theirs)


def first_kernel(
    plane_ref, beta_ref, succ_ref, sets_ref, emis_hbm, trans_hbm,
    out_ref, pick_ref, own_ref, flip_ref,
    emis_ref, trans, choose, total, arrived,
):
    emis_load = pltpu.make_async_copy(emis_hbm, emis_ref, arrived.at[0])
    trans_load = pltpu.make_async_copy(trans_hbm, trans, arrived.at[1])
    emis_load.start()
    trans_load.start()
    states, width = beta_ref.shape
    lanes = own_ref.shape[1]
    for j in range(DEG):
        at = slice(j * states, (j + 1) * states)
        pick_ref[at] = (iota((states, states), 1) == succ_ref[:, j : j + 1]).astype(BF)
        choose[at] = (iota((states, NSET), 1) == sets_ref[:, j : j + 1]).astype(BF)
    emis_load.wait()
    mine = emis_ref[:, pl.ds(pl.multiple_of(plane_ref[0] * lanes, lanes), lanes)].astype(F32).T.astype(BF)
    for j in range(DEG):
        own_ref[j] = dot(mine, choose[j * states : (j + 1) * states], ROWS).astype(BF)
    for b in range(width // BLK):
        cols = slice(b * BLK, (b + 1) * BLK)
        mixed = jnp.zeros((states, BLK), F32)
        for j in range(DEG):
            at = slice(j * states, (j + 1) * states)
            mixed = mixed + dot(pick_ref[at], beta_ref[:, cols]) * dot(choose[at], emis_ref[:, cols])
        if b == 0:
            trans_load.wait()
        flip_ref[b] = trans[cols].T
        part = dot(flip_ref[b], mixed.astype(BF), ROWS)
        total[...] = part if b == 0 else total[...] + part
    for i in range(4):
        for z in range(4):
            at = z * 4 + i
            out_ref[i, z * 64 : (z + 1) * 64] = total[at * 64 : (at + 1) * 64].astype(BF)


def mix_and_multiply(plane, beta, succ, sets, emis, trans):
    states = beta.shape[0]
    width, outs = trans.shape
    return pl.pallas_call(
        first_kernel,
        out_shape=(
            shape((4, outs // 4, states)),
            shape((DEG * states, states)),
            shape((DEG, 128, states)),
            shape((width // BLK, outs, BLK)),
        ),
        in_specs=[SCALAR] + [WHOLE] * 3 + [pl.BlockSpec(memory_space=pl.ANY)] * 2,
        out_specs=(WHOLE,) * 4,
        scratch_shapes=[
            pltpu.VMEM((NSET, width), BF),
            pltpu.VMEM((width, outs), BF),
            pltpu.VMEM((DEG * states, NSET), BF),
            pltpu.VMEM((outs, states), F32),
            pltpu.SemaphoreType.DMA((2,)),
        ],
        compiler_params=params(BIG),
        name="mix_multiply",
    )(plane, beta, succ, sets, emis, trans)


def near_kernel(parts_ref, out_ref):
    total = parts_ref[0].astype(F32)
    for i in range(1, 4):
        total = total + parts_ref[i].astype(F32)
    for i in range(2):
        out_ref[i] = total.astype(BF)


def near_sum(parts):
    _, rows, states = parts.shape
    return pl.pallas_call(
        near_kernel, out_shape=shape((2, rows, states)), compiler_params=params(16), name="near_sum"
    )(parts)


def half_place(states):
    return (states >> 3 & 1) * 128 + (states >> 4) * 8 + (states & 7)


def middle_kernel(zh_ref, parts_ref, pick_ref, own_ref, out_ref, keep_ref):
    pieces = []
    for s in range(2):
        total = parts_ref[4 * s].astype(F32)
        for i in range(1, 4):
            total = total + parts_ref[4 * s + i].astype(F32)
        pieces.append(total)
    beta = jnp.concatenate(pieces, 0).astype(BF)
    states = beta.shape[1]
    mixed = jnp.zeros(beta.shape, F32)
    for j in range(DEG):
        mixed = mixed + dot(beta, pick_ref[j * states : (j + 1) * states], ROWS) * own_ref[j].astype(F32)
    place = half_place(iota((states, states), 0))
    order = (iota((states, states), 1) == place).astype(BF)
    mixed = dot(mixed.astype(BF), order).astype(BF)
    for i in range(out_ref.shape[0]):
        out_ref[i] = mixed
    half = states // 2
    place = half_place(iota((states, half), 0)) - zh_ref[0] * half
    mine = (iota((states, half), 1) == place).astype(BF)
    keep_ref[...] = dot(beta, mine).astype(BF)


def sum_and_mix(zh, parts, pick, own):
    _, cells, states = parts.shape
    return pl.pallas_call(
        middle_kernel,
        out_shape=(shape((16, 2 * cells, states)), shape((2 * cells, states // 2))),
        in_specs=[SCALAR, WHOLE, WHOLE, WHOLE],
        compiler_params=params(16),
        name="sum_mix",
    )(zh, parts, pick, own)


def second_kernel(mixed_ref, trans_ref, out_ref):
    for z in range(0, 8, 2):
        rows = slice(z * 128, (z + 2) * 128)
        part = dot(trans_ref[0, rows], mixed_ref[:BLK])
        for i in range(1, trans_ref.shape[0]):
            part = part + dot(trans_ref[i, rows], mixed_ref[i * BLK : (i + 1) * BLK])
        for i in range(4):
            for s in range(2):
                out_ref[i % 2, s, z + i // 2] = part[i * 64 : (i + 1) * 64, s * 128 : (s + 1) * 128]


def multiply(mixed, trans):
    return pl.pallas_call(
        second_kernel,
        out_shape=shape((2, 2, 8, 64, 128), F32),
        in_specs=[WHOLE] * 2,
        out_specs=WHOLE,
        compiler_params=params(16),
        name="multiply",
    )(mixed, trans)


def last_kernel(parts_ref, keep_ref, out_ref):
    pieces = []
    for s in range(2):
        total = parts_ref[8 * s].astype(F32)
        for i in range(1, 8):
            total = total + parts_ref[8 * s + i].astype(F32)
        pieces.append(total)
    pieces.append(keep_ref[...].astype(F32))
    out_ref[...] = jnp.concatenate(pieces, 0).T.astype(BF).reshape(out_ref.shape)


def sum_and_join(parts, keep):
    _, cells, half = parts.shape
    return pl.pallas_call(
        last_kernel,
        out_shape=shape((half // 8, 8, 4 * cells)),
        compiler_params=params(16),
        name="sum_join",
    )(parts, keep)


def local(beta_last, transition, emission, successor, token_set):
    states, blocks, _, cells = beta_last.shape
    width = blocks * cells
    zh = jnp.full((1,), lax.axis_index("zh"), jnp.int32)
    plane = jnp.full((1,), lax.axis_index("y") * 4 + lax.axis_index("x"), jnp.int32)

    mine = as_rows(beta_last.reshape(states, blocks, cells))
    theirs = lax.ppermute(mine, "zh", [(0, 1), (1, 0)])
    beta = lax.all_to_all(pair_copies(zh, mine, theirs), PLANE, 0, 0).reshape(256, width)

    partial, pick, own, trans = mix_and_multiply(
        plane, beta, successor, token_set, emission.reshape(NSET, width), transition.reshape(width, -1)
    )
    near = near_sum(lax.all_to_all(partial, ("z0", "c"), 0, 0))
    parts = lax.all_to_all(near.reshape(8, cells, 256), ("zh", "z2", "z1"), 0, 0)
    copies, keep = sum_and_mix(zh, parts, pick, own)
    mixed = lax.all_to_all(copies, PLANE, 0, 0).reshape(width, 256)

    pair = lax.all_to_all(multiply(mixed, trans), "c", 0, 0)
    halves = (pair[0] + pair[1]).astype(BF).reshape(16, cells, 128)
    parts = lax.all_to_all(halves, ("zh", "z2", "z1", "z0"), 0, 0)
    moved = lax.all_to_all(sum_and_join(parts, keep), PLANE, 0, 0)
    moved = moved.reshape(16, states, 2, 2, cells).transpose(2, 1, 0, 3, 4)
    return moved.reshape(2, states, blocks, 1, cells)


def solution(mesh):
    fine = Mesh(mesh.devices.reshape(4, 4, 2, 2, 2, 2, 2), ("y", "x", "zh", "z2", "z1", "z0", "c"))
    dfa, hid = ("y", "x", "zh"), ("z2", "z1", "z0", "c")
    return jax.shard_map(
        local,
        mesh=fine,
        in_specs=(
            P(dfa, None, hid, None),
            P(None, hid, None, dfa),
            P(None, hid, None),
            P(),
            P(),
        ),
        out_specs=P(None, dfa, None, hid, None),
        check_vma=False,
    )
```

```python
import jax
import jax.numpy as jnp
from jax import lax
from jax.experimental import pallas as pl
from jax.experimental.pallas import tpu as pltpu
from jax.sharding import Mesh, PartitionSpec as P

BF, F32 = jnp.bfloat16, jnp.float32
DEG, NSET = 8, 64
PLANE = ("y", "x")
MIB = 1024 * 1024
BLK = 256
BIG = 45
WHOLE = pl.BlockSpec(memory_space=pltpu.VMEM)
SCALAR = pl.BlockSpec(memory_space=pltpu.SMEM)


def shape(dims, dtype=BF):
    return jax.ShapeDtypeStruct(dims, dtype)


def params(mib):
    return pltpu.CompilerParams(vmem_limit_bytes=mib * MIB)


def dot(a, b, dims=((1,), (0,))):
    return lax.dot_general(a, b, (dims, ((), ())), preferred_element_type=F32)


ROWS = ((1,), (1,))


def iota(dims, axis):
    return lax.broadcasted_iota(jnp.int32, dims, axis)


def rows_kernel(beta_ref, out_ref):
    for i in range(0, beta_ref.shape[1], 2):
        out_ref[:, i * 64 : (i + 2) * 64] = jnp.concatenate([beta_ref[:, i], beta_ref[:, i + 1]], 1)


def as_rows(beta):
    states, blocks, cells = beta.shape
    return pl.pallas_call(
        rows_kernel, out_shape=shape((states, blocks * cells)), compiler_params=params(16), name="as_rows"
    )(beta)


def copies_kernel(rows_ref, out_ref):
    rows = rows_ref[...].astype(F32).reshape(out_ref.shape[1:]).astype(BF)
    for i in range(out_ref.shape[0]):
        out_ref[i] = rows


def copies_of(rows):
    _, states, width = rows.shape
    return pl.pallas_call(
        copies_kernel, out_shape=shape((16, 2 * states, width)), compiler_params=params(16), name="copies"
    )(rows)


def tables_kernel(place_ref, succ_ref, sets_ref, emis_ref, trans_ref, pick_ref, choose_ref, own_ref, flip_ref):
    states = succ_ref.shape[0]
    lanes = own_ref.shape[1]
    mine = emis_ref[:, pl.ds(pl.multiple_of(place_ref[0] * lanes, lanes), lanes)].astype(F32).T.astype(BF)
    for j in range(DEG):
        at = slice(j * states, (j + 1) * states)
        pick_ref[at] = (iota((states, states), 1) == succ_ref[:, j : j + 1]).astype(BF)
        choose = (iota((states, NSET), 1) == sets_ref[:, j : j + 1]).astype(BF)
        choose_ref[at] = choose
        own_ref[j] = dot(mine, choose, ROWS).astype(BF)
    for b in range(flip_ref.shape[0]):
        flip_ref[b] = trans_ref[b * BLK : (b + 1) * BLK].T


def tables(place, succ, sets, emis, trans):
    states = succ.shape[0]
    width, outs = trans.shape
    return pl.pallas_call(
        tables_kernel,
        out_shape=(
            shape((DEG * states, states)),
            shape((DEG * states, NSET)),
            shape((DEG, 128, states)),
            shape((width // BLK, outs, BLK)),
        ),
        in_specs=[SCALAR] + [WHOLE] * 4,
        out_specs=(WHOLE,) * 4,
        compiler_params=params(16),
        cost_estimate=pl.CostEstimate(flops=2**31, bytes_accessed=12 * MIB, transcendentals=0),
        name="tables",
    )(place, succ, sets, emis, trans)


def first_kernel(beta_ref, pick_ref, choose_ref, emis_ref, flip_hbm, out_ref, flip_ref, mixed_at, total, arrived):
    load = pltpu.make_async_copy(flip_hbm, flip_ref, arrived)
    load.start()
    states, width = beta_ref.shape
    for b in range(width // BLK):
        cols = slice(b * BLK, (b + 1) * BLK)
        mixed = jnp.zeros((states, BLK), F32)
        for j in range(DEG):
            at = slice(j * states, (j + 1) * states)
            mixed = mixed + dot(pick_ref[at], beta_ref[:, cols]) * dot(choose_ref[at], emis_ref[:, cols])
        mixed_at[b] = mixed.astype(BF)
    load.wait()
    for b in range(width // BLK):
        part = dot(flip_ref[b], mixed_at[b], ROWS)
        total[...] = part if b == 0 else total[...] + part
    for i in range(4):
        for z in range(4):
            at = z * 4 + i
            out_ref[i, z * 64 : (z + 1) * 64] = total[at * 64 : (at + 1) * 64].astype(BF)


def mix_and_multiply(beta, pick, choose, emis, flip):
    states = beta.shape[0]
    blocks, outs, _ = flip.shape
    return pl.pallas_call(
        first_kernel,
        out_shape=(shape((4, outs // 4, states)), shape(flip.shape)),
        in_specs=[WHOLE] * 4 + [pl.BlockSpec(memory_space=pl.ANY)],
        out_specs=(WHOLE,) * 2,
        scratch_shapes=[
            pltpu.VMEM((blocks, states, BLK), BF),
            pltpu.VMEM((outs, states), F32),
            pltpu.SemaphoreType.DMA(()),
        ],
        compiler_params=params(BIG),
        name="mix_multiply",
    )(beta, pick, choose, emis, flip)


def near_kernel(parts_ref, out_ref):
    total = parts_ref[0].astype(F32)
    for i in range(1, 4):
        total = total + parts_ref[i].astype(F32)
    for i in range(2):
        out_ref[i] = total.astype(BF)


def near_sum(parts):
    _, rows, states = parts.shape
    return pl.pallas_call(
        near_kernel, out_shape=shape((2, rows, states)), compiler_params=params(16), name="near_sum"
    )(parts)


def half_place(states):
    return (states >> 3 & 1) * 128 + (states >> 4) * 8 + (states & 7)


def middle_kernel(place_ref, parts_ref, pick_ref, own_ref, out_ref, keep_ref):
    pieces = []
    for s in range(2):
        total = parts_ref[4 * s].astype(F32)
        for i in range(1, 4):
            total = total + parts_ref[4 * s + i].astype(F32)
        pieces.append(total)
    beta = jnp.concatenate(pieces, 0).astype(BF)
    states = beta.shape[1]
    mixed = jnp.zeros(beta.shape, F32)
    for j in range(DEG):
        mixed = mixed + dot(beta, pick_ref[j * states : (j + 1) * states], ROWS) * own_ref[j].astype(F32)
    place = half_place(iota((states, states), 0))
    order = (iota((states, states), 1) == place).astype(BF)
    mixed = dot(mixed.astype(BF), order).astype(BF)
    for i in range(out_ref.shape[0]):
        out_ref[i] = mixed
    half = states // 2
    place = half_place(iota((states, half), 0)) - place_ref[1] * half
    mine = (iota((states, half), 1) == place).astype(BF)
    keep_ref[...] = dot(beta, mine).astype(BF)


def sum_and_mix(place, parts, pick, own):
    _, cells, states = parts.shape
    return pl.pallas_call(
        middle_kernel,
        out_shape=(shape((16, 2 * cells, states)), shape((2 * cells, states // 2))),
        in_specs=[SCALAR, WHOLE, WHOLE, WHOLE],
        compiler_params=params(16),
        name="sum_mix",
    )(place, parts, pick, own)


def second_kernel(mixed_ref, trans_ref, out_ref):
    for z in range(0, 8, 2):
        rows = slice(z * 128, (z + 2) * 128)
        part = dot(trans_ref[0, rows], mixed_ref[:BLK])
        for i in range(1, trans_ref.shape[0]):
            part = part + dot(trans_ref[i, rows], mixed_ref[i * BLK : (i + 1) * BLK])
        for i in range(4):
            for s in range(2):
                out_ref[i % 2, s, z + i // 2] = part[i * 64 : (i + 1) * 64, s * 128 : (s + 1) * 128]


def multiply(mixed, trans):
    return pl.pallas_call(
        second_kernel,
        out_shape=shape((2, 2, 8, 64, 128), F32),
        in_specs=[WHOLE] * 2,
        out_specs=WHOLE,
        compiler_params=params(16),
        name="multiply",
    )(mixed, trans)


def last_kernel(parts_ref, keep_ref, out_ref):
    pieces = []
    for s in range(2):
        total = parts_ref[8 * s].astype(F32)
        for i in range(1, 8):
            total = total + parts_ref[8 * s + i].astype(F32)
        pieces.append(total)
    pieces.append(keep_ref[...].astype(F32))
    out_ref[...] = jnp.concatenate(pieces, 0).T.astype(BF).reshape(out_ref.shape)


def sum_and_join(parts, keep):
    _, cells, half = parts.shape
    return pl.pallas_call(
        last_kernel,
        out_shape=shape((half // 8, 8, 4 * cells)),
        compiler_params=params(16),
        name="sum_join",
    )(parts, keep)


def local(beta_last, transition, emission, successor, token_set):
    states, blocks, _, cells = beta_last.shape
    width = blocks * cells
    place = jnp.stack([lax.axis_index("y") * 4 + lax.axis_index("x"), lax.axis_index("zh")])

    mine = as_rows(beta_last.reshape(states, blocks, cells))
    pair = lax.all_gather(mine, "zh", axis=0)
    beta = lax.all_to_all(copies_of(pair), PLANE, 0, 0).reshape(256, width)
    emis = emission.reshape(NSET, width)
    pick, choose, own, flipped = tables(place, successor, token_set, emis, transition.reshape(width, -1))
    partial, trans = mix_and_multiply(beta, pick, choose, emis, flipped)
    near = near_sum(lax.all_to_all(partial, ("z0", "c"), 0, 0))
    parts = lax.all_to_all(near.reshape(8, cells, 256), ("zh", "z2", "z1"), 0, 0)
    copies, keep = sum_and_mix(place, parts, pick, own)
    mixed = lax.all_to_all(copies, PLANE, 0, 0).reshape(width, 256)

    pair = lax.all_to_all(multiply(mixed, trans), "c", 0, 0)
    halves = (pair[0] + pair[1]).astype(BF).reshape(16, cells, 128)
    parts = lax.all_to_all(halves, ("zh", "z2", "z1", "z0"), 0, 0)
    moved = lax.all_to_all(sum_and_join(parts, keep), PLANE, 0, 0)
    moved = moved.reshape(16, states, 2, 2, cells).transpose(2, 1, 0, 3, 4)
    return moved.reshape(2, states, blocks, 1, cells)


def solution(mesh):
    fine = Mesh(mesh.devices.reshape(4, 4, 2, 2, 2, 2, 2), ("y", "x", "zh", "z2", "z1", "z0", "c"))
    dfa, hid = ("y", "x", "zh"), ("z2", "z1", "z0", "c")
    return jax.shard_map(
        local,
        mesh=fine,
        in_specs=(
            P(dfa, None, hid, None),
            P(None, hid, None, dfa),
            P(None, hid, None),
            P(),
            P(),
        ),
        out_specs=P(None, dfa, None, hid, None),
        check_vma=False,
    )
```

```python
import jax
import jax.numpy as jnp
from jax import lax
from jax.experimental import pallas as pl
from jax.experimental.pallas import tpu as pltpu
from jax.sharding import Mesh, PartitionSpec as P

BF, F32 = jnp.bfloat16, jnp.float32
DEG, NSET = 8, 64
PLANE = ("y", "x")
MIB = 1024 * 1024
BLK = 256
BIG = 45
WHOLE = pl.BlockSpec(memory_space=pltpu.VMEM)
SCALAR = pl.BlockSpec(memory_space=pltpu.SMEM)


def shape(dims, dtype=BF):
    return jax.ShapeDtypeStruct(dims, dtype)


def params(mib):
    return pltpu.CompilerParams(vmem_limit_bytes=mib * MIB)


def dot(a, b, dims=((1,), (0,))):
    return lax.dot_general(a, b, (dims, ((), ())), preferred_element_type=F32)


ROWS = ((1,), (1,))


def iota(dims, axis):
    return lax.broadcasted_iota(jnp.int32, dims, axis)


def rows_kernel(beta_ref, out_ref):
    for i in range(0, beta_ref.shape[1], 2):
        out_ref[:, i * 64 : (i + 2) * 64] = jnp.concatenate([beta_ref[:, i], beta_ref[:, i + 1]], 1)


def as_rows(beta):
    states, blocks, cells = beta.shape
    return pl.pallas_call(
        rows_kernel, out_shape=shape((states, blocks * cells)), compiler_params=params(16), name="as_rows"
    )(beta)


def copies_kernel(rows_ref, out_ref):
    rows = rows_ref[...].astype(F32).reshape(out_ref.shape[1:]).astype(BF)
    for i in range(out_ref.shape[0]):
        out_ref[i] = rows


def copies_of(rows):
    _, states, width = rows.shape
    return pl.pallas_call(
        copies_kernel, out_shape=shape((16, 2 * states, width)), compiler_params=params(16), name="copies"
    )(rows)


def tables_kernel(place_ref, succ_ref, sets_ref, emis_ref, trans_ref, pick_ref, choose_ref, own_ref, flip_ref):
    states = succ_ref.shape[0]
    lanes = own_ref.shape[1]
    mine = emis_ref[:, pl.ds(pl.multiple_of(place_ref[0] * lanes, lanes), lanes)].astype(F32).T.astype(BF)
    for j in range(DEG):
        at = slice(j * states, (j + 1) * states)
        pick_ref[at] = (iota((states, states), 1) == succ_ref[:, j : j + 1]).astype(BF)
        choose = (iota((states, NSET), 1) == sets_ref[:, j : j + 1]).astype(BF)
        choose_ref[at] = choose
        own_ref[j] = dot(mine, choose, ROWS).astype(BF)
    for b in range(flip_ref.shape[0]):
        flip_ref[b] = trans_ref[b * BLK : (b + 1) * BLK].T


def tables(place, succ, sets, emis, trans):
    states = succ.shape[0]
    width, outs = trans.shape
    return pl.pallas_call(
        tables_kernel,
        out_shape=(
            shape((DEG * states, states)),
            shape((DEG * states, NSET)),
            shape((DEG, 128, states)),
            shape((width // BLK, outs, BLK)),
        ),
        in_specs=[SCALAR] + [WHOLE] * 4,
        out_specs=(WHOLE,) * 4,
        compiler_params=params(16),
        cost_estimate=pl.CostEstimate(flops=2**31, bytes_accessed=12 * MIB, transcendentals=0),
        name="tables",
    )(place, succ, sets, emis, trans)


def first_kernel(beta_ref, pick_ref, choose_ref, emis_ref, flip_hbm, out_ref, flip_ref, mixed_at, total, arrived):
    load = pltpu.make_async_copy(flip_hbm, flip_ref, arrived)
    load.start()
    states, width = beta_ref.shape
    for b in range(width // BLK):
        cols = slice(b * BLK, (b + 1) * BLK)
        mixed = jnp.zeros((states, BLK), F32)
        for j in range(DEG):
            at = slice(j * states, (j + 1) * states)
            mixed = mixed + dot(pick_ref[at], beta_ref[:, cols]) * dot(choose_ref[at], emis_ref[:, cols])
        mixed_at[b] = mixed.astype(BF)
    load.wait()
    for b in range(width // BLK):
        part = dot(flip_ref[b], mixed_at[b], ROWS)
        total[...] = part if b == 0 else total[...] + part
    for i in range(4):
        for z in range(4):
            at = z * 4 + i
            out_ref[i, z * 64 : (z + 1) * 64] = total[at * 64 : (at + 1) * 64].astype(BF)


def mix_and_multiply(beta, pick, choose, emis, flip):
    states = beta.shape[0]
    blocks, outs, _ = flip.shape
    return pl.pallas_call(
        first_kernel,
        out_shape=(shape((4, outs // 4, states)), shape(flip.shape)),
        in_specs=[WHOLE] * 4 + [pl.BlockSpec(memory_space=pl.ANY)],
        out_specs=(WHOLE,) * 2,
        scratch_shapes=[
            pltpu.VMEM((blocks, states, BLK), BF),
            pltpu.VMEM((outs, states), F32),
            pltpu.SemaphoreType.DMA(()),
        ],
        compiler_params=params(BIG),
        name="mix_multiply",
    )(beta, pick, choose, emis, flip)


def near_kernel(parts_ref, out_ref):
    total = parts_ref[0].astype(F32)
    for i in range(1, 4):
        total = total + parts_ref[i].astype(F32)
    cells = out_ref.shape[1]
    for i in range(out_ref.shape[0]):
        out_ref[i] = total[i // 2 * cells : (i // 2 + 1) * cells].astype(BF)


def near_sum(parts):
    _, rows, states = parts.shape
    return pl.pallas_call(
        near_kernel, out_shape=shape((8, rows // 4, states)), compiler_params=params(16), name="near_sum"
    )(parts)


def half_place(states):
    return (states >> 3 & 1) * 128 + (states >> 4) * 8 + (states & 7)


def middle_kernel(place_ref, parts_ref, pick_ref, own_ref, out_ref, keep_ref):
    pieces = []
    for s in range(2):
        total = parts_ref[s].astype(F32)
        for i in range(1, 4):
            total = total + parts_ref[2 * i + s].astype(F32)
        pieces.append(total)
    beta = jnp.concatenate(pieces, 0).astype(BF)
    states = beta.shape[1]
    mixed = jnp.zeros(beta.shape, F32)
    for j in range(DEG):
        mixed = mixed + dot(beta, pick_ref[j * states : (j + 1) * states], ROWS) * own_ref[j].astype(F32)
    place = half_place(iota((states, states), 0))
    order = (iota((states, states), 1) == place).astype(BF)
    mixed = dot(mixed.astype(BF), order).astype(BF)
    for i in range(out_ref.shape[0]):
        out_ref[i] = mixed
    half = states // 2
    place = half_place(iota((states, half), 0)) - place_ref[1] * half
    mine = (iota((states, half), 1) == place).astype(BF)
    keep_ref[...] = dot(beta, mine).astype(BF)


def sum_and_mix(place, parts, pick, own):
    _, cells, states = parts.shape
    return pl.pallas_call(
        middle_kernel,
        out_shape=(shape((16, 2 * cells, states)), shape((2 * cells, states // 2))),
        in_specs=[SCALAR, WHOLE, WHOLE, WHOLE],
        compiler_params=params(16),
        name="sum_mix",
    )(place, parts, pick, own)


def second_kernel(place_ref, mixed_ref, trans_ref, keep_ref, send_ref):
    first = place_ref[2] == 0
    for z in range(4):
        rows = slice(z * 256, (z + 1) * 256)
        part = dot(trans_ref[0, rows], mixed_ref[:BLK])
        for i in range(1, trans_ref.shape[0]):
            part = part + dot(trans_ref[i, rows], mixed_ref[i * BLK : (i + 1) * BLK])
        for i in range(2):
            for s in range(2):
                lanes = slice(s * 128, (s + 1) * 128)
                a, b = part[i * 128 : i * 128 + 64, lanes], part[i * 128 + 64 : (i + 1) * 128, lanes]
                keep_ref[s * 8 + z * 2 + i] = jnp.where(first, a, b)
                send_ref[s * 8 + z * 2 + i] = jnp.where(first, b, a).astype(BF)


def multiply(place, mixed, trans):
    return pl.pallas_call(
        second_kernel,
        out_shape=(shape((16, 64, 128), F32), shape((16, 64, 128))),
        in_specs=[SCALAR] + [WHOLE] * 2,
        out_specs=(WHOLE,) * 2,
        compiler_params=params(16),
        name="multiply",
    )(place, mixed, trans)


def last_kernel(parts_ref, keep_ref, out_ref):
    pieces = []
    for s in range(2):
        total = parts_ref[8 * s].astype(F32)
        for i in range(1, 8):
            total = total + parts_ref[8 * s + i].astype(F32)
        pieces.append(total)
    pieces.append(keep_ref[...].astype(F32))
    out_ref[...] = jnp.concatenate(pieces, 0).T.astype(BF).reshape(out_ref.shape)


def sum_and_join(parts, keep):
    _, cells, half = parts.shape
    return pl.pallas_call(
        last_kernel,
        out_shape=shape((half // 8, 8, 4 * cells)),
        compiler_params=params(16),
        name="sum_join",
    )(parts, keep)


def local(beta_last, transition, emission, successor, token_set):
    states, blocks, _, cells = beta_last.shape
    width = blocks * cells
    plane = lax.axis_index("y") * 4 + lax.axis_index("x")
    place = jnp.stack([plane, lax.axis_index("zh"), lax.axis_index("c")])

    mine = as_rows(beta_last.reshape(states, blocks, cells))
    pair = lax.all_gather(mine, "zh", axis=0)
    beta = lax.all_to_all(copies_of(pair), PLANE, 0, 0).reshape(256, width)
    emis = emission.reshape(NSET, width)
    pick, choose, own, flipped = tables(place, successor, token_set, emis, transition.reshape(width, -1))
    partial, trans = mix_and_multiply(beta, pick, choose, emis, flipped)
    near = near_sum(lax.all_to_all(partial, ("z0", "c"), 0, 0))
    parts = lax.all_to_all(near, ("z2", "z1", "zh"), 0, 0)
    copies, keep = sum_and_mix(place, parts, pick, own)
    mixed = lax.all_to_all(copies, PLANE, 0, 0).reshape(width, 256)

    kept, send = multiply(place, mixed, trans)
    halves = (kept + lax.ppermute(send, "c", [(0, 1), (1, 0)]).astype(F32)).astype(BF)
    parts = lax.all_to_all(halves, ("zh", "z2", "z1", "z0"), 0, 0)
    moved = lax.all_to_all(sum_and_join(parts, keep), PLANE, 0, 0)
    moved = moved.reshape(16, states, 2, 2, cells).transpose(2, 1, 0, 3, 4)
    return moved.reshape(2, states, blocks, 1, cells)


def solution(mesh):
    fine = Mesh(mesh.devices.reshape(4, 4, 2, 2, 2, 2, 2), ("y", "x", "zh", "z2", "z1", "z0", "c"))
    dfa, hid = ("y", "x", "zh"), ("z2", "z1", "z0", "c")
    return jax.shard_map(
        local,
        mesh=fine,
        in_specs=(
            P(dfa, None, hid, None),
            P(None, hid, None, dfa),
            P(None, hid, None),
            P(),
            P(),
        ),
        out_specs=P(None, dfa, None, hid, None),
        check_vma=False,
    )
```

```python
import jax
import jax.numpy as jnp
from jax import lax
from jax.experimental import pallas as pl
from jax.experimental.pallas import tpu as pltpu
from jax.sharding import Mesh, PartitionSpec as P

BF, F32 = jnp.bfloat16, jnp.float32
DEG, NSET = 8, 64
PLANE = ("y", "x")
MIB = 1024 * 1024
BLK = 256
BIG = 45
WHOLE = pl.BlockSpec(memory_space=pltpu.VMEM)
SCALAR = pl.BlockSpec(memory_space=pltpu.SMEM)


def shape(dims, dtype=BF):
    return jax.ShapeDtypeStruct(dims, dtype)


def params(mib):
    return pltpu.CompilerParams(vmem_limit_bytes=mib * MIB)


def dot(a, b, dims=((1,), (0,))):
    return lax.dot_general(a, b, (dims, ((), ())), preferred_element_type=F32)


ROWS = ((1,), (1,))


def iota(dims, axis):
    return lax.broadcasted_iota(jnp.int32, dims, axis)


def rows_kernel(beta_ref, out_ref):
    for i in range(0, beta_ref.shape[1], 2):
        out_ref[:, i * 64 : (i + 2) * 64] = jnp.concatenate([beta_ref[:, i], beta_ref[:, i + 1]], 1)


def as_rows(beta):
    states, blocks, cells = beta.shape
    return pl.pallas_call(
        rows_kernel, out_shape=shape((states, blocks * cells)), compiler_params=params(16), name="as_rows"
    )(beta)


def copies_kernel(rows_ref, out_ref):
    rows = rows_ref[...].astype(F32).reshape(out_ref.shape[1:]).astype(BF)
    for i in range(out_ref.shape[0]):
        out_ref[i] = rows


def copies_of(rows):
    _, states, width = rows.shape
    return pl.pallas_call(
        copies_kernel, out_shape=shape((16, 2 * states, width)), compiler_params=params(16), name="copies"
    )(rows)


def tables_kernel(place_ref, succ_ref, sets_ref, emis_ref, trans_ref, pick_ref, choose_ref, own_ref, flip_ref):
    states = succ_ref.shape[0]
    lanes = own_ref.shape[1]
    mine = emis_ref[:, pl.ds(pl.multiple_of(place_ref[0] * lanes, lanes), lanes)].astype(F32).T.astype(BF)
    for j in range(DEG):
        at = slice(j * states, (j + 1) * states)
        pick_ref[at] = (iota((states, states), 1) == succ_ref[:, j : j + 1]).astype(BF)
        choose = (iota((states, NSET), 1) == sets_ref[:, j : j + 1]).astype(BF)
        choose_ref[at] = choose
        own_ref[j] = dot(mine, choose, ROWS).astype(BF)
    for b in range(flip_ref.shape[0]):
        flip_ref[b] = trans_ref[b * BLK : (b + 1) * BLK].T


def tables(place, succ, sets, emis, trans):
    states = succ.shape[0]
    width, outs = trans.shape
    return pl.pallas_call(
        tables_kernel,
        out_shape=(
            shape((DEG * states, states)),
            shape((DEG * states, NSET)),
            shape((DEG, 128, states)),
            shape((width // BLK, outs, BLK)),
        ),
        in_specs=[SCALAR] + [WHOLE] * 4,
        out_specs=(WHOLE,) * 4,
        compiler_params=params(16),
        cost_estimate=pl.CostEstimate(flops=2**31, bytes_accessed=12 * MIB, transcendentals=0),
        name="tables",
    )(place, succ, sets, emis, trans)


def first_kernel(beta_ref, pick_ref, choose_ref, emis_ref, flip_hbm, out_ref, flip_ref, mixed_at, total, arrived):
    load = pltpu.make_async_copy(flip_hbm, flip_ref, arrived)
    load.start()
    states, width = beta_ref.shape
    for b in range(width // BLK):
        cols = slice(b * BLK, (b + 1) * BLK)
        mixed = jnp.zeros((states, BLK), F32)
        for j in range(DEG):
            at = slice(j * states, (j + 1) * states)
            mixed = mixed + dot(pick_ref[at], beta_ref[:, cols]) * dot(choose_ref[at], emis_ref[:, cols])
        mixed_at[b] = mixed.astype(BF)
    load.wait()
    for b in range(width // BLK):
        part = dot(flip_ref[b], mixed_at[b], ROWS)
        total[...] = part if b == 0 else total[...] + part
    for i in range(4):
        for z in range(4):
            at = z * 4 + i
            out_ref[i, z * 64 : (z + 1) * 64] = total[at * 64 : (at + 1) * 64].astype(BF)


def mix_and_multiply(beta, pick, choose, emis, flip):
    states = beta.shape[0]
    blocks, outs, _ = flip.shape
    return pl.pallas_call(
        first_kernel,
        out_shape=(shape((4, outs // 4, states)), shape(flip.shape)),
        in_specs=[WHOLE] * 4 + [pl.BlockSpec(memory_space=pl.ANY)],
        out_specs=(WHOLE,) * 2,
        scratch_shapes=[
            pltpu.VMEM((blocks, states, BLK), BF),
            pltpu.VMEM((outs, states), F32),
            pltpu.SemaphoreType.DMA(()),
        ],
        compiler_params=params(BIG),
        name="mix_multiply",
    )(beta, pick, choose, emis, flip)


def near_kernel(parts_ref, out_ref):
    total = parts_ref[0].astype(F32)
    for i in range(1, 4):
        total = total + parts_ref[i].astype(F32)
    cells = out_ref.shape[1]
    for i in range(out_ref.shape[0]):
        out_ref[i] = total[i // 2 * cells : (i // 2 + 1) * cells].astype(BF)


def near_sum(parts):
    _, rows, states = parts.shape
    return pl.pallas_call(
        near_kernel, out_shape=shape((8, rows // 4, states)), compiler_params=params(16), name="near_sum"
    )(parts)


def half_place(states):
    return (states >> 3 & 1) * 128 + (states >> 4) * 8 + (states & 7)


def middle_kernel(parts_ref, pick_ref, own_ref, out_ref, keep_ref):
    pieces = []
    for s in range(2):
        total = parts_ref[s].astype(F32)
        for i in range(1, 4):
            total = total + parts_ref[2 * i + s].astype(F32)
        pieces.append(total)
    beta = jnp.concatenate(pieces, 0).astype(BF)
    states = beta.shape[1]
    mixed = jnp.zeros(beta.shape, F32)
    for j in range(DEG):
        mixed = mixed + dot(beta, pick_ref[j * states : (j + 1) * states], ROWS) * own_ref[j].astype(F32)
    place = half_place(iota((states, states), 0))
    order = (iota((states, states), 1) == place).astype(BF)
    mixed = dot(mixed.astype(BF), order).astype(BF)
    for i in range(out_ref.shape[0]):
        out_ref[i] = mixed
    half = states // 2
    place = half_place(iota((states, half), 0)) - lax.axis_index("zh") * half
    mine = (iota((states, half), 1) == place).astype(BF)
    keep_ref[...] = dot(beta, mine).astype(BF)


def sum_and_mix(parts, pick, own):
    _, cells, states = parts.shape
    return pl.pallas_call(
        middle_kernel,
        out_shape=(shape((16, 2 * cells, states)), shape((2 * cells, states // 2))),
        in_specs=[WHOLE] * 3,
        compiler_params=params(16),
        name="sum_mix",
    )(parts, pick, own)


def second_kernel(mixed_ref, trans_ref, keep_ref, send_ref):
    first = lax.axis_index("c") == 0
    for z in range(4):
        rows = slice(z * 256, (z + 1) * 256)
        part = dot(trans_ref[0, rows], mixed_ref[:BLK])
        for i in range(1, trans_ref.shape[0]):
            part = part + dot(trans_ref[i, rows], mixed_ref[i * BLK : (i + 1) * BLK])
        for i in range(2):
            for s in range(2):
                lanes = slice(s * 128, (s + 1) * 128)
                a, b = part[i * 128 : i * 128 + 64, lanes], part[i * 128 + 64 : (i + 1) * 128, lanes]
                keep_ref[s * 8 + z * 2 + i] = jnp.where(first, a, b)
                send_ref[s * 8 + z * 2 + i] = jnp.where(first, b, a).astype(BF)


def multiply(mixed, trans):
    return pl.pallas_call(
        second_kernel,
        out_shape=(shape((16, 64, 128), F32), shape((16, 64, 128))),
        in_specs=[WHOLE] * 2,
        out_specs=(WHOLE,) * 2,
        compiler_params=params(16),
        name="multiply",
    )(mixed, trans)


def last_kernel(parts_ref, keep_ref, out_ref):
    pieces = []
    for s in range(2):
        total = parts_ref[8 * s].astype(F32)
        for i in range(1, 8):
            total = total + parts_ref[8 * s + i].astype(F32)
        pieces.append(total)
    pieces.append(keep_ref[...].astype(F32))
    out_ref[...] = jnp.concatenate(pieces, 0).T.astype(BF).reshape(out_ref.shape)


def sum_and_join(parts, keep):
    _, cells, half = parts.shape
    return pl.pallas_call(
        last_kernel,
        out_shape=shape((half // 8, 8, 4 * cells)),
        compiler_params=params(16),
        name="sum_join",
    )(parts, keep)


def local(beta_last, transition, emission, successor, token_set):
    states, blocks, _, cells = beta_last.shape
    width = blocks * cells
    plane = lax.axis_index("y") * 4 + lax.axis_index("x")
    place = jnp.full((1,), plane, jnp.int32)

    mine = as_rows(beta_last.reshape(states, blocks, cells))
    pair = lax.all_gather(mine, "zh", axis=0)
    beta = lax.all_to_all(copies_of(pair), PLANE, 0, 0).reshape(256, width)
    emis = emission.reshape(NSET, width)
    pick, choose, own, flipped = tables(place, successor, token_set, emis, transition.reshape(width, -1))
    partial, trans = mix_and_multiply(beta, pick, choose, emis, flipped)
    near = near_sum(lax.all_to_all(partial, ("z0", "c"), 0, 0))
    parts = lax.all_to_all(near, ("z2", "z1", "zh"), 0, 0)
    copies, keep = sum_and_mix(parts, pick, own)
    mixed = lax.all_to_all(copies, PLANE, 0, 0).reshape(width, 256)

    kept, send = multiply(mixed, trans)
    halves = (kept + lax.ppermute(send, "c", [(0, 1), (1, 0)]).astype(F32)).astype(BF)
    parts = lax.all_to_all(halves, ("zh", "z2", "z1", "z0"), 0, 0)
    moved = lax.all_to_all(sum_and_join(parts, keep), PLANE, 0, 0)
    moved = moved.reshape(16, states, 2, 2, cells).transpose(2, 1, 0, 3, 4)
    return moved.reshape(2, states, blocks, 1, cells)


def solution(mesh):
    fine = Mesh(mesh.devices.reshape(4, 4, 2, 2, 2, 2, 2), ("y", "x", "zh", "z2", "z1", "z0", "c"))
    dfa, hid = ("y", "x", "zh"), ("z2", "z1", "z0", "c")
    return jax.shard_map(
        local,
        mesh=fine,
        in_specs=(
            P(dfa, None, hid, None),
            P(None, hid, None, dfa),
            P(None, hid, None),
            P(),
            P(),
        ),
        out_specs=P(None, dfa, None, hid, None),
        check_vma=False,
    )
```

```python
import jax
import jax.numpy as jnp
from jax import lax
from jax.experimental import pallas as pl
from jax.experimental.pallas import tpu as pltpu
from jax.sharding import Mesh, PartitionSpec as P

BF, F32 = jnp.bfloat16, jnp.float32
DEG, NSET = 8, 64
PLANE = ("y", "x")
MIB = 1024 * 1024
BLK = 256
BIG = 45
WHOLE = pl.BlockSpec(memory_space=pltpu.VMEM)
SCALAR = pl.BlockSpec(memory_space=pltpu.SMEM)


def shape(dims, dtype=BF):
    return jax.ShapeDtypeStruct(dims, dtype)


def params(mib):
    return pltpu.CompilerParams(vmem_limit_bytes=mib * MIB)


def dot(a, b, dims=((1,), (0,))):
    return lax.dot_general(a, b, (dims, ((), ())), preferred_element_type=F32)


ROWS = ((1,), (1,))


def iota(dims, axis):
    return lax.broadcasted_iota(jnp.int32, dims, axis)


def rows_kernel(beta_ref, out_ref):
    for i in range(0, beta_ref.shape[1], 2):
        out_ref[:, i * 64 : (i + 2) * 64] = jnp.concatenate([beta_ref[:, i], beta_ref[:, i + 1]], 1)


def as_rows(beta):
    states, blocks, cells = beta.shape
    return pl.pallas_call(
        rows_kernel, out_shape=shape((states, blocks * cells)), compiler_params=params(16), name="as_rows"
    )(beta)


def copies_kernel(rows_ref, out_ref):
    rows = rows_ref[...].astype(F32).reshape(out_ref.shape[1:]).astype(BF)
    for i in range(out_ref.shape[0]):
        out_ref[i] = rows


def copies_of(rows):
    _, states, width = rows.shape
    return pl.pallas_call(
        copies_kernel, out_shape=shape((16, 2 * states, width)), compiler_params=params(16), name="copies"
    )(rows)


def tables_kernel(place_ref, succ_ref, sets_ref, emis_ref, trans_ref, pick_ref, choose_ref, own_ref, flip_ref):
    states = succ_ref.shape[0]
    lanes = own_ref.shape[1]
    mine = emis_ref[:, pl.ds(pl.multiple_of(place_ref[0] * lanes, lanes), lanes)].astype(F32).T.astype(BF)
    for j in range(DEG):
        at = slice(j * states, (j + 1) * states)
        pick_ref[at] = (iota((states, states), 1) == succ_ref[:, j : j + 1]).astype(BF)
        choose = (iota((states, NSET), 1) == sets_ref[:, j : j + 1]).astype(BF)
        choose_ref[at] = choose
        own_ref[j] = dot(mine, choose, ROWS).astype(BF)
    for b in range(flip_ref.shape[0]):
        flip_ref[b] = trans_ref[b * BLK : (b + 1) * BLK].T


def tables(place, succ, sets, emis, trans):
    states = succ.shape[0]
    width, outs = trans.shape
    return pl.pallas_call(
        tables_kernel,
        out_shape=(
            shape((DEG * states, states)),
            shape((DEG * states, NSET)),
            shape((DEG, 128, states)),
            shape((width // BLK, outs, BLK)),
        ),
        in_specs=[SCALAR] + [WHOLE] * 4,
        out_specs=(WHOLE,) * 4,
        compiler_params=params(16),
        cost_estimate=pl.CostEstimate(flops=2**31, bytes_accessed=12 * MIB, transcendentals=0),
        name="tables",
    )(place, succ, sets, emis, trans)


def first_kernel(beta_ref, pick_ref, choose_ref, emis_ref, flip_hbm, out_ref, flip_ref, mixed_at, total, arrived):
    load = pltpu.make_async_copy(flip_hbm, flip_ref, arrived)
    load.start()
    states, width = beta_ref.shape
    for b in range(width // BLK):
        cols = slice(b * BLK, (b + 1) * BLK)
        mixed = jnp.zeros((states, BLK), F32)
        for j in range(0, DEG, 2):
            at = slice(j * states, (j + 2) * states)
            both = dot(pick_ref[at], beta_ref[:, cols]) * dot(choose_ref[at], emis_ref[:, cols])
            mixed = mixed + both[:states] + both[states:]
        mixed_at[b] = mixed.astype(BF)
    load.wait()
    for b in range(width // BLK):
        part = dot(flip_ref[b], mixed_at[b], ROWS)
        total[...] = part if b == 0 else total[...] + part
    for i in range(4):
        for z in range(4):
            at = z * 4 + i
            out_ref[i, z * 64 : (z + 1) * 64] = total[at * 64 : (at + 1) * 64].astype(BF)


def mix_and_multiply(beta, pick, choose, emis, flip):
    states = beta.shape[0]
    blocks, outs, _ = flip.shape
    return pl.pallas_call(
        first_kernel,
        out_shape=(shape((4, outs // 4, states)), shape(flip.shape)),
        in_specs=[WHOLE] * 4 + [pl.BlockSpec(memory_space=pl.ANY)],
        out_specs=(WHOLE,) * 2,
        scratch_shapes=[
            pltpu.VMEM((blocks, states, BLK), BF),
            pltpu.VMEM((outs, states), F32),
            pltpu.SemaphoreType.DMA(()),
        ],
        compiler_params=params(BIG),
        name="mix_multiply",
    )(beta, pick, choose, emis, flip)


def near_kernel(parts_ref, out_ref):
    total = parts_ref[0].astype(F32)
    for i in range(1, 4):
        total = total + parts_ref[i].astype(F32)
    cells = out_ref.shape[1]
    for i in range(out_ref.shape[0]):
        out_ref[i] = total[i // 2 * cells : (i // 2 + 1) * cells].astype(BF)


def near_sum(parts):
    _, rows, states = parts.shape
    return pl.pallas_call(
        near_kernel, out_shape=shape((8, rows // 4, states)), compiler_params=params(16), name="near_sum"
    )(parts)


def half_place(states):
    return (states >> 3 & 1) * 128 + (states >> 4) * 8 + (states & 7)


def middle_kernel(parts_ref, pick_ref, own_ref, out_ref, keep_ref):
    pieces = []
    for s in range(2):
        total = parts_ref[s].astype(F32)
        for i in range(1, 4):
            total = total + parts_ref[2 * i + s].astype(F32)
        pieces.append(total)
    beta = jnp.concatenate(pieces, 0).astype(BF)
    states = beta.shape[1]
    mixed = jnp.zeros(beta.shape, F32)
    for j in range(DEG):
        mixed = mixed + dot(beta, pick_ref[j * states : (j + 1) * states], ROWS) * own_ref[j].astype(F32)
    place = half_place(iota((states, states), 0))
    order = (iota((states, states), 1) == place).astype(BF)
    mixed = dot(mixed.astype(BF), order).astype(BF)
    for i in range(out_ref.shape[0]):
        out_ref[i] = mixed
    half = states // 2
    place = half_place(iota((states, half), 0)) - lax.axis_index("zh") * half
    mine = (iota((states, half), 1) == place).astype(BF)
    keep_ref[...] = dot(beta, mine).astype(BF)


def sum_and_mix(parts, pick, own):
    _, cells, states = parts.shape
    return pl.pallas_call(
        middle_kernel,
        out_shape=(shape((16, 2 * cells, states)), shape((2 * cells, states // 2))),
        in_specs=[WHOLE] * 3,
        compiler_params=params(16),
        name="sum_mix",
    )(parts, pick, own)


def second_kernel(mixed_ref, trans_ref, keep_ref, send_ref):
    first = lax.axis_index("c") == 0
    for z in range(4):
        rows = slice(z * 256, (z + 1) * 256)
        part = dot(trans_ref[0, rows], mixed_ref[:BLK])
        for i in range(1, trans_ref.shape[0]):
            part = part + dot(trans_ref[i, rows], mixed_ref[i * BLK : (i + 1) * BLK])
        for i in range(2):
            for s in range(2):
                lanes = slice(s * 128, (s + 1) * 128)
                a, b = part[i * 128 : i * 128 + 64, lanes], part[i * 128 + 64 : (i + 1) * 128, lanes]
                keep_ref[s * 8 + z * 2 + i] = jnp.where(first, a, b)
                send_ref[s * 8 + z * 2 + i] = jnp.where(first, b, a).astype(BF)


def multiply(mixed, trans):
    return pl.pallas_call(
        second_kernel,
        out_shape=(shape((16, 64, 128), F32), shape((16, 64, 128))),
        in_specs=[WHOLE] * 2,
        out_specs=(WHOLE,) * 2,
        compiler_params=params(16),
        name="multiply",
    )(mixed, trans)


def last_kernel(parts_ref, keep_ref, out_ref):
    pieces = []
    for s in range(2):
        total = parts_ref[8 * s].astype(F32)
        for i in range(1, 8):
            total = total + parts_ref[8 * s + i].astype(F32)
        pieces.append(total)
    pieces.append(keep_ref[...].astype(F32))
    out_ref[...] = jnp.concatenate(pieces, 0).T.astype(BF).reshape(out_ref.shape)


def sum_and_join(parts, keep):
    _, cells, half = parts.shape
    return pl.pallas_call(
        last_kernel,
        out_shape=shape((half // 8, 8, 4 * cells)),
        compiler_params=params(16),
        name="sum_join",
    )(parts, keep)


def local(beta_last, transition, emission, successor, token_set):
    states, blocks, _, cells = beta_last.shape
    width = blocks * cells
    plane = lax.axis_index("y") * 4 + lax.axis_index("x")
    place = jnp.full((1,), plane, jnp.int32)

    mine = as_rows(beta_last.reshape(states, blocks, cells))
    pair = lax.all_gather(mine, "zh", axis=0)
    beta = lax.all_to_all(copies_of(pair), PLANE, 0, 0).reshape(256, width)
    emis = emission.reshape(NSET, width)
    pick, choose, own, flipped = tables(place, successor, token_set, emis, transition.reshape(width, -1))
    partial, trans = mix_and_multiply(beta, pick, choose, emis, flipped)
    near = near_sum(lax.all_to_all(partial, ("z0", "c"), 0, 0))
    parts = lax.all_to_all(near, ("z2", "z1", "zh"), 0, 0)
    copies, keep = sum_and_mix(parts, pick, own)
    mixed = lax.all_to_all(copies, PLANE, 0, 0).reshape(width, 256)

    kept, send = multiply(mixed, trans)
    halves = (kept + lax.ppermute(send, "c", [(0, 1), (1, 0)]).astype(F32)).astype(BF)
    parts = lax.all_to_all(halves, ("zh", "z2", "z1", "z0"), 0, 0)
    moved = lax.all_to_all(sum_and_join(parts, keep), PLANE, 0, 0)
    moved = moved.reshape(16, states, 2, 2, cells).transpose(2, 1, 0, 3, 4)
    return moved.reshape(2, states, blocks, 1, cells)


def solution(mesh):
    fine = Mesh(mesh.devices.reshape(4, 4, 2, 2, 2, 2, 2), ("y", "x", "zh", "z2", "z1", "z0", "c"))
    dfa, hid = ("y", "x", "zh"), ("z2", "z1", "z0", "c")
    return jax.shard_map(
        local,
        mesh=fine,
        in_specs=(
            P(dfa, None, hid, None),
            P(None, hid, None, dfa),
            P(None, hid, None),
            P(),
            P(),
        ),
        out_specs=P(None, dfa, None, hid, None),
        check_vma=False,
    )
```
